512 devices in a mesh: occ: 64 (over z_lo, y, core), aux: 8 (over x, z_hi).
Axes of the slice: x: 4, y: 4, z: 16 (z_hi: 2, z_lo: 8; z = z_hi * 8 + z_lo), core: 2. Of those that a mesh axis runs over, the one named last changes fastest.
Arguments:
- half_blocks: bfloat16 [1536, 64, 6144], P('occ', None, 'aux'), may hold values from -0.796875 to 0.796875
- block_rows: int32 [64], replicated, may hold values from 1 to 24, 768 in all
- block_order: int32 [64], replicated, may hold values from 0 to 63, each once
- ao_to_virt: bfloat16 [768, 512], replicated, may hold values from -0.21875 to 0.21875
- occ_energy: float32 [64], replicated, may hold values from -2 to -0.5
- virt_energy: float32 [512], replicated, may hold values from 0.2 to 3
Outputs:
- gamma: float32 [64, 512, 6144], P('occ', None, 'aux')
The draws below stay inside these ranges and needn't reach their ends.
Inputs may be any that keep to these rules, and one draw needn't show every extreme that they name: block_rows[s] is the number of AO functions held by device s of occ; the counts sum to 768 and one of them equals 24. A permutation; the runs of AO functions lie end to end in the order of block_order.
All inputs are finite; a program needn't handle non-finite values.
Results may differ from the reference program's by a relative error of at most 0.008.
Values may be sent and summed in bfloat16 or wider, within the bound.
No kernel may reach another device: no remote copies, remote signals or barrier semaphores. Data moves between devices by JAX's collectives and lax.ppermute only.
A program may use at most 64 MiB of HBM per device.

```python
import math
import jax
import jax.numpy as jnp
import numpy as np
from jax import lax

VT = 512
MAXROWS = 24
CYCLE = 3
NOCC = 64
NAUX = 6144
AO_WIN = 768
N_OCC = 64


def block_levels(key, extent, shards, smallest, largest):
    gain, own = 1.0, jax.random.fold_in(key, 6)
    for dim, blocks in shards:
        heights = jnp.exp(jax.random.uniform(jax.random.fold_in(own, dim), (blocks,), jnp.float32, smallest / len(shards), largest / len(shards)))
        gain = gain * jnp.repeat(heights, extent[dim] // blocks).reshape([-1 if axis == dim else 1 for axis in range(len(extent))])
    return gain


def profile(count, total, reach, skew):
    weights = [(1 << 20) // math.isqrt(grade ** skew) + 1 for grade in range(2, count + 1)]
    rest, holding = total - reach - (count - 1), [1] * (count - 1)
    while rest > 0:
        movable = [i for i in range(count - 1) if holding[i] < reach]
        pool, left = sum([weights[i] for i in movable]), rest
        for i in movable:
            addition = min(reach - holding[i], max(1, left * weights[i] // pool), rest)
            holding[i] = holding[i] + addition
            rest = rest - addition
    return np.array([reach] + holding)


def uneven(key, amount, total, bound, lean):
    if amount == 2:
        one = jax.random.randint(key, (), max(1, total - bound), min(bound, total - 1) + 1)
        return jnp.stack([one, total - one])
    tallies = jnp.asarray(profile(amount, total, bound, lean), jnp.int32)
    twos = (amount - 1) // 2
    giver, receiver = tallies[1:1 + 2 * twos:2], tallies[2:2 + 2 * twos:2]
    room = jnp.minimum(giver - 1, bound - receiver)
    passed = jax.random.randint(jax.random.fold_in(key, 1), (twos,), 0, 1 << 20) % (room + 1)
    tallies = tallies.at[1:1 + 2 * twos:2].set(giver - passed).at[2:2 + 2 * twos:2].set(receiver + passed)
    return tallies[jax.random.permutation(jax.random.fold_in(key, 2), amount)]


def bell_draw(key, shape, spread, reach, pieces=(), kind=jnp.bfloat16):
    level = block_levels(key, shape, pieces, -0.22, 0.18) if pieces else 1.0
    entries = jax.random.normal(key, shape, jnp.float32) * spread * level
    return jnp.minimum(jnp.maximum(entries, -reach), reach).astype(kind)


def setup_inputs(seed: int = 0) -> dict:
    arg_keys = jax.random.split(jax.random.key(seed), 7)
    half_blocks = bell_draw(arg_keys[0], (N_OCC * MAXROWS, NOCC, NAUX), 0.1, 0.796875, ((0, 64), (2, 8)))
    block_rows = uneven(arg_keys[1], N_OCC, AO_WIN, MAXROWS, 2).astype(jnp.int32)
    block_order = jax.random.permutation(arg_keys[2], N_OCC).astype(jnp.int32)
    ao_to_virt = bell_draw(arg_keys[3], (AO_WIN, VT), AO_WIN ** -0.5, 0.21875)
    occ_energy = jnp.clip(jax.random.uniform(arg_keys[4], (NOCC,), jnp.float32, -2.0, -0.5), -2.0, -0.5)
    virt_energy = jnp.clip(jax.random.uniform(arg_keys[5], (VT,), jnp.float32, 0.2, 3.0), 0.2, 3.0)
    return dict(half_blocks=half_blocks, block_rows=block_rows, block_order=block_order, ao_to_virt=ao_to_virt, occ_energy=occ_energy, virt_energy=virt_energy)


def build_table(block_rows, block_order, ao_to_virt, maxrows):
    device_count = block_rows.shape[0]
    matches = block_order[:, None] == jnp.arange(device_count, dtype=jnp.int32)[None, :]
    ordered = jnp.sum(jnp.where(matches, block_rows[None, :], 0), axis=1).astype(jnp.int32)
    before = (jnp.cumsum(ordered) - ordered).astype(jnp.int32)
    starts = jnp.sum(jnp.where(matches, before[:, None], 0), axis=0).astype(jnp.int32)
    offset = jnp.arange(maxrows, dtype=jnp.int32)
    in_block = offset[None, :] < block_rows[:, None]
    row_index = jnp.where(in_block, starts[:, None] + offset[None, :], 0).reshape(-1).astype(jnp.int32)
    ao_rows = jnp.take(ao_to_virt, row_index, axis=0)
    return jnp.where(in_block.reshape(-1, 1), ao_rows, jnp.zeros_like(ao_rows))


def contract_rows(ao_table, received):
    return lax.dot_general(ao_table, received, (((0,), (0,)), ((), ())), preferred_element_type=jnp.float32).astype(jnp.bfloat16)


def reference(half_blocks, block_rows, block_order, ao_to_virt, occ_energy, virt_energy):
    device_count = block_rows.shape[0]
    maxrows = half_blocks.shape[0] // device_count
    ao_table = build_table(block_rows, block_order, ao_to_virt, maxrows)
    occ_count = occ_energy.shape[0]

    def one_tile(index):
        return contract_rows(ao_table, lax.dynamic_index_in_dim(half_blocks, index, 1, keepdims=False))

    virt_tiles = lax.map(one_tile, jnp.arange(occ_count, dtype=jnp.int32))

    def one_gamma(index):
        own_tile = lax.dynamic_index_in_dim(virt_tiles, index, 0, keepdims=False)
        density = jnp.zeros((own_tile.shape[0], own_tile.shape[1]), jnp.float32)
        for cycle_step in range(CYCLE + 1):
            partner = ((index - cycle_step) % occ_count).astype(jnp.int32)
            other_tile = lax.dynamic_index_in_dim(virt_tiles, partner, 0, keepdims=False)
            product = lax.dot_general(own_tile, other_tile, (((1,), (1,)), ((), ())), preferred_element_type=jnp.float32)
            merged = 2.0 * product - product.T
            energy_gap = virt_energy[:, None] + virt_energy[None, :] - occ_energy[index] - occ_energy[partner]
            amplitudes = (merged / energy_gap).astype(jnp.bfloat16)
            density = density + jnp.dot(amplitudes, other_tile, preferred_element_type=jnp.float32)
        return density

    return lax.map(one_gamma, jnp.arange(occ_count, dtype=jnp.int32))
```

```python
import functools

import jax
import jax.numpy as jnp
from jax import lax
from jax.experimental import pallas as pl
from jax.experimental.pallas import tpu as pltpu
from jax.sharding import PartitionSpec as P

CYCLE = 3
XS = 4
ZS = 2


def shifted(value, axis, by):
    devices = lax.axis_size(axis)
    return lax.ppermute(value, axis, [(i, (i + by) % devices) for i in range(devices)])


def shifted_x(value, by):
    perm = [(x * ZS + z, (x + by) % XS * ZS + z) for x in range(XS) for z in range(ZS)]
    return lax.ppermute(value, "aux", perm)


def swapped_z(value):
    perm = [(x * ZS + z, x * ZS + 1 - z) for x in range(XS) for z in range(ZS)]
    return lax.ppermute(value, "aux", perm)


def ao_layout(block_rows, block_order, maxrows):
    device_count = block_rows.shape[0]
    matches = block_order[:, None] == jnp.arange(device_count, dtype=jnp.int32)[None, :]
    ordered = jnp.sum(jnp.where(matches, block_rows[None, :], 0), axis=1)
    before = jnp.cumsum(ordered) - ordered
    starts = jnp.sum(jnp.where(matches, before[:, None], 0), axis=0)
    offset = jnp.arange(maxrows, dtype=jnp.int32)
    in_block = offset[None, :] < block_rows[:, None]
    target = starts[:, None] + offset[None, :]
    return (in_block, target)


def build_table(block_rows, block_order, ao_to_virt, maxrows):
    in_block, target = ao_layout(block_rows, block_order, maxrows)
    row_index = jnp.where(in_block, target, 0).reshape(-1)
    ao_rows = jnp.take(ao_to_virt, row_index, axis=0)
    return jnp.where(in_block.reshape(-1, 1), ao_rows, jnp.zeros_like(ao_rows))


def contract_rows(ao_table, received):
    return lax.dot_general(
        ao_table, received, (((0,), (0,)), ((), ())), preferred_element_type=jnp.float32
    ).astype(jnp.bfloat16)


NT = (((1,), (1,)), ((), ()))
IN_VMEM = pl.BlockSpec(memory_space=pltpu.VMEM)
IN_SMEM = pl.BlockSpec(memory_space=pltpu.SMEM)


def grant(mib):
    return pltpu.CompilerParams(vmem_limit_bytes=mib << 20)


def pair_kernel(x_ref, own_ref, other_ref, *out_refs):
    rows = out_refs[0].shape[0]
    x = x_ref[0]
    for step, out_ref in enumerate(out_refs):
        block = pl.ds(pl.multiple_of(lax.rem(x + step, XS) * rows, rows), rows)
        direct = lax.dot_general(
            own_ref[block, :], other_ref[...], NT, preferred_element_type=jnp.float32
        )
        crossed = lax.dot_general(
            other_ref[block, :], own_ref[...], NT, preferred_element_type=jnp.float32
        )
        out_ref[...] = (2.0 * direct - crossed).astype(out_ref.dtype)


def pair_blocks(x, own, other):
    vt, columns = own.shape
    rows = vt // XS
    return pl.pallas_call(
        pair_kernel,
        out_shape=[jax.ShapeDtypeStruct((rows, vt), jnp.bfloat16)] * XS,
        in_specs=[IN_SMEM, IN_VMEM, IN_VMEM],
        out_specs=[IN_VMEM] * XS,
        compiler_params=grant(6),
        cost_estimate=pl.CostEstimate(
            flops=4 * vt * vt * columns, bytes_accessed=4 * vt * columns + 2 * vt * vt, transcendentals=0
        ),
    )(x, own, other)


def sum_kernel(*refs):
    total = refs[0][...].astype(jnp.float32)
    for ref in refs[1:-1]:
        total = total + ref[...].astype(jnp.float32)
    refs[-1][...] = total.astype(refs[-1].dtype)


def sum_of(*blocks):
    size = blocks[0].size
    return pl.pallas_call(
        sum_kernel,
        out_shape=jax.ShapeDtypeStruct(blocks[0].shape, jnp.bfloat16),
        in_specs=[IN_VMEM] * len(blocks),
        out_specs=IN_VMEM,
        compiler_params=grant(4),
        cost_estimate=pl.CostEstimate(
            flops=len(blocks) * size, bytes_accessed=2 * (len(blocks) + 1) * size, transcendentals=0
        ),
    )(*blocks)


def amplitude_kernel(energy_ref, column_ref, row_ref, one_ref, two_ref, out_ref):
    merged = one_ref[...].astype(jnp.float32) + two_ref[...].astype(jnp.float32)
    gap = column_ref[...] + row_ref[...] - energy_ref[0] - energy_ref[1]
    out_ref[...] = (merged / gap).astype(out_ref.dtype)


def amplitude_of(energies, column, row, one, two):
    return pl.pallas_call(
        amplitude_kernel,
        out_shape=jax.ShapeDtypeStruct(one.shape, jnp.bfloat16),
        in_specs=[IN_SMEM] + [IN_VMEM] * 4,
        out_specs=IN_VMEM,
        compiler_params=grant(4),
        cost_estimate=pl.CostEstimate(
            flops=6 * one.size, bytes_accessed=6 * one.size, transcendentals=0
        ),
    )(energies, column, row, one, two)


def density_kernel(count, x_ref, *refs):
    blocks, tiles, rest = refs[: count * XS], refs[count * XS : count * (XS + 1)], refs[count * (XS + 1) :]
    out_ref = rest[-1]
    rows = blocks[0].shape[0]
    x = x_ref[0]
    for step in range(XS):
        block = pl.ds(pl.multiple_of(lax.rem(x + XS - step, XS) * rows, rows), rows)
        total = rest[0][block, :] if len(rest) > 1 else None
        for k in range(count):
            term = jnp.dot(blocks[k * XS + step][...], tiles[k][...], preferred_element_type=jnp.float32)
            total = term if total is None else total + term
        out_ref[block, :] = total


def density_of(x, amplitudes, tiles, so_far=None):
    count = len(tiles)
    vt, columns = tiles[0].shape
    args = [x] + [block for blocks in amplitudes for block in blocks] + list(tiles)
    aliases = {}
    if so_far is not None:
        aliases = {len(args): 0}
        args.append(so_far)
    return pl.pallas_call(
        functools.partial(density_kernel, count),
        out_shape=jax.ShapeDtypeStruct((vt, columns), jnp.float32),
        in_specs=[IN_SMEM] + [IN_VMEM] * (len(args) - 1),
        out_specs=IN_VMEM,
        compiler_params=grant(16),
        input_output_aliases=aliases,
        cost_estimate=pl.CostEstimate(
            flops=2 * count * vt * vt * columns,
            bytes_accessed=4 * vt * columns + count * (2 * vt * columns + 2 * vt * vt),
            transcendentals=0,
        ),
    )(*args)


def shards(half_blocks, block_rows, block_order, ao_to_virt, occ_energy, virt_energy):
    maxrows = half_blocks.shape[0]
    device_count = occ_energy.shape[0]
    vt = ao_to_virt.shape[1]
    rows = vt // XS
    position = lax.axis_index("occ")
    x = lax.axis_index("aux") // ZS
    x_arg = jnp.reshape(x, (1,)).astype(jnp.int32)
    ao_table = build_table(block_rows, block_order, ao_to_virt, maxrows)
    own_tile = contract_rows(
        ao_table,
        lax.all_to_all(half_blocks, "occ", split_axis=1, concat_axis=0, tiled=True)[:, 0, :],
    )
    column = lax.dynamic_slice_in_dim(virt_energy, x * rows, rows)[:, None]
    row = virt_energy[None, :]
    tiles = [own_tile]
    for _ in range(CYCLE):
        tiles.append(shifted(tiles[-1], "occ", 1))
    amplitudes = []
    for cycle_step in range(CYCLE + 1):
        partner = (position - cycle_step) % device_count
        energies = jnp.stack([occ_energy[position], occ_energy[partner]])
        blocks = pair_blocks(x_arg, own_tile, tiles[cycle_step])
        part = sum_of(blocks[0], *(shifted_x(blocks[step], step) for step in range(1, XS)))
        amplitude = amplitude_of(energies, column, row, part, swapped_z(part))
        amplitudes.append([amplitude] + [shifted_x(amplitude, step) for step in range(1, XS)])
    density = density_of(x_arg, amplitudes[:CYCLE], tiles[:CYCLE])
    return density_of(x_arg, amplitudes[CYCLE:], tiles[CYCLE:], density)[None]


def solution(mesh):
    return jax.shard_map(
        shards,
        mesh=mesh,
        in_specs=(P("occ", None, "aux"), P(), P(), P(), P(), P()),
        out_specs=P("occ", None, "aux"),
        check_vma=False,
    )
```

```python
import functools

import jax
import jax.numpy as jnp
from jax import lax
from jax.experimental import pallas as pl
from jax.experimental.pallas import tpu as pltpu
from jax.sharding import PartitionSpec as P


XS = 4
ZS = 2


def shifted(value, axis, by):
    devices = lax.axis_size(axis)
    return lax.ppermute(value, axis, [(i, (i + by) % devices) for i in range(devices)])


def exchanged_x(value):
    groups = [[x * ZS + z for x in range(XS)] for z in range(ZS)]
    return lax.all_to_all(value, "aux", 0, 0, axis_index_groups=groups, tiled=True)


def swapped_z(value):
    perm = [(x * ZS + z, x * ZS + 1 - z) for x in range(XS) for z in range(ZS)]
    return lax.ppermute(value, "aux", perm)


def ao_layout(block_rows, block_order, maxrows):
    device_count = block_rows.shape[0]
    matches = block_order[:, None] == jnp.arange(device_count, dtype=jnp.int32)[None, :]
    ordered = jnp.sum(jnp.where(matches, block_rows[None, :], 0), axis=1)
    before = jnp.cumsum(ordered) - ordered
    starts = jnp.sum(jnp.where(matches, before[:, None], 0), axis=0)
    offset = jnp.arange(maxrows, dtype=jnp.int32)
    in_block = offset[None, :] < block_rows[:, None]
    target = starts[:, None] + offset[None, :]
    return (in_block, target)


def build_table(block_rows, block_order, ao_to_virt, maxrows):
    in_block, target = ao_layout(block_rows, block_order, maxrows)
    row_index = jnp.where(in_block, target, 0).reshape(-1)
    ao_rows = jnp.take(ao_to_virt, row_index, axis=0)
    return jnp.where(in_block.reshape(-1, 1), ao_rows, jnp.zeros_like(ao_rows))


def contract_rows(ao_table, received):
    return lax.dot_general(
        ao_table, received, (((0,), (0,)), ((), ())), preferred_element_type=jnp.float32
    ).astype(jnp.bfloat16)


NT = (((1,), (1,)), ((), ()))
IN_VMEM = pl.BlockSpec(memory_space=pltpu.VMEM)
IN_SMEM = pl.BlockSpec(memory_space=pltpu.SMEM)


def grant(mib):
    return pltpu.CompilerParams(vmem_limit_bytes=mib << 20)


def pair_kernel(own_ref, *refs):
    others, out_ref = refs[:-1], refs[-1]
    copies, _, rows, _ = out_ref.shape
    for step in range(copies):
        block = pl.ds(step * rows, rows)
        for k, other_ref in enumerate(others):
            direct = lax.dot_general(
                own_ref[block, :], other_ref[...], NT, preferred_element_type=jnp.float32
            )
            crossed = lax.dot_general(
                other_ref[block, :], own_ref[...], NT, preferred_element_type=jnp.float32
            )
            out_ref[step, k] = (2.0 * direct - crossed).astype(out_ref.dtype)


def pair_blocks(own, others):
    vt, columns = own.shape
    count = len(others)
    return pl.pallas_call(
        pair_kernel,
        out_shape=jax.ShapeDtypeStruct((XS, count, vt // XS, vt), jnp.bfloat16),
        in_specs=[IN_VMEM] * (1 + count),
        out_specs=IN_VMEM,
        compiler_params=grant(4 + 2 * count),
        cost_estimate=pl.CostEstimate(
            flops=4 * count * vt * vt * columns,
            bytes_accessed=2 * (1 + count) * vt * columns + 2 * count * vt * vt,
            transcendentals=0,
        ),
    )(own, *others)


def sum_kernel(blocks_ref, out_ref):
    total = blocks_ref[0].astype(jnp.float32)
    for step in range(1, blocks_ref.shape[0]):
        total = total + blocks_ref[step].astype(jnp.float32)
    out_ref[...] = total.astype(out_ref.dtype)


def sum_of(blocks):
    return pl.pallas_call(
        sum_kernel,
        out_shape=jax.ShapeDtypeStruct(blocks.shape[1:], jnp.bfloat16),
        in_specs=[IN_VMEM],
        out_specs=IN_VMEM,
        compiler_params=grant(4),
        cost_estimate=pl.CostEstimate(
            flops=blocks.size, bytes_accessed=3 * blocks.size, transcendentals=0
        ),
    )(blocks)


def amplitude_kernel(steps, place_ref, energy_ref, column_ref, row_ref, one_ref, two_ref, out_ref):
    copies, _, rows, _ = out_ref.shape
    occupied = energy_ref.shape[0]
    position = place_ref[0]
    block = pl.ds(pl.multiple_of(place_ref[1] * rows, rows), rows)
    both = column_ref[block, :] + row_ref[...]
    for k, step in enumerate(steps):
        partner = lax.rem(position + occupied - step, occupied)
        gap = both - energy_ref[position] - energy_ref[partner]
        merged = one_ref[k].astype(jnp.float32) + two_ref[k].astype(jnp.float32)
        amplitude = (merged / gap).astype(out_ref.dtype)
        for copy in range(copies):
            out_ref[copy, k] = amplitude


def amplitude_of(steps, place, energies, column, row, one, two):
    return pl.pallas_call(
        functools.partial(amplitude_kernel, steps),
        out_shape=jax.ShapeDtypeStruct((XS,) + one.shape, jnp.bfloat16),
        in_specs=[IN_SMEM] * 2 + [IN_VMEM] * 4,
        out_specs=IN_VMEM,
        compiler_params=grant(6),
        cost_estimate=pl.CostEstimate(
            flops=6 * one.size, bytes_accessed=12 * one.size, transcendentals=0
        ),
    )(place, energies, column, row, one, two)


def density_kernel(counts, *refs):
    amplitudes, tiles = refs[: len(counts)], refs[len(counts) : len(counts) + sum(counts)]
    rest = refs[len(counts) + sum(counts) :]
    out_ref = rest[-1]
    steps, _, rows, _ = amplitudes[0].shape
    pairs = [(ref, k) for ref, count in zip(amplitudes, counts) for k in range(count)]
    for step in range(steps):
        block = pl.ds(step * rows, rows)
        total = rest[0][block, :] if len(rest) > 1 else None
        for (ref, k), tile in zip(pairs, tiles):
            term = jnp.dot(ref[step, k], tile[...], preferred_element_type=jnp.float32)
            total = term if total is None else total + term
        out_ref[block, :] = total


def density_of(amplitudes, tiles, so_far=None):
    counts = [a.shape[1] for a in amplitudes]
    count = sum(counts)
    vt, columns = tiles[0].shape
    args = list(amplitudes) + list(tiles)
    aliases = {}
    if so_far is not None:
        aliases = {len(args): 0}
        args.append(so_far)
    return pl.pallas_call(
        functools.partial(density_kernel, counts),
        out_shape=jax.ShapeDtypeStruct((vt, columns), jnp.float32),
        in_specs=[IN_VMEM] * len(args),
        out_specs=IN_VMEM,
        compiler_params=grant(12),
        input_output_aliases=aliases,
        cost_estimate=pl.CostEstimate(
            flops=2 * count * vt * vt * columns,
            bytes_accessed=4 * vt * columns + count * (2 * vt * columns + 2 * vt * vt),
            transcendentals=0,
        ),
    )(*args)


GROUPS = ((0,), (1, 2), (3,))


def shards(half_blocks, block_rows, block_order, ao_to_virt, occ_energy, virt_energy):
    maxrows = half_blocks.shape[0]
    place = jnp.stack([lax.axis_index("occ"), lax.axis_index("aux") // ZS]).astype(jnp.int32)
    column, row = virt_energy[:, None], virt_energy[None, :]
    ao_table = build_table(block_rows, block_order, ao_to_virt, maxrows)
    own_tile = contract_rows(
        ao_table,
        lax.all_to_all(half_blocks, "occ", split_axis=1, concat_axis=0, tiled=True)[:, 0, :],
    )
    tiles = [own_tile, shifted(own_tile, "occ", 1), shifted(own_tile, "occ", 2)]
    tiles.append(shifted(tiles[2], "occ", 1))
    amplitudes = []
    for steps in GROUPS:
        blocks = pair_blocks(own_tile, [tiles[k] for k in steps])
        received = exchanged_x(blocks)
        part = sum_of(received)
        other = swapped_z(part)
        amplitude = amplitude_of(steps, place, occ_energy, column, row, part, other)
        amplitudes.append(exchanged_x(amplitude))
    density = density_of(amplitudes[:2], tiles[:3])
    return density_of(amplitudes[2:], tiles[3:], density)[None]


def solution(mesh):
    return jax.shard_map(
        shards,
        mesh=mesh,
        in_specs=(P("occ", None, "aux"), P(), P(), P(), P(), P()),
        out_specs=P("occ", None, "aux"),
        check_vma=False,
    )
```

```python
import functools
import math

import jax
import jax.numpy as jnp
from jax import lax
from jax.experimental import pallas as pl
from jax.experimental.pallas import tpu as pltpu
from jax.sharding import PartitionSpec as P


XS = 4
ZS = 2
PLANE = 8
DIRECT = 8
STEADY = 80


def shifted(value, axis, by):
    devices = lax.axis_size(axis)
    return lax.ppermute(value, axis, [(i, (i + by) % devices) for i in range(devices)])


def exchanged_x(value):
    groups = [[x * ZS + z for x in range(XS)] for z in range(ZS)]
    return lax.all_to_all(value, "aux", 0, 0, axis_index_groups=groups, tiled=True)


def swapped_z(value):
    perm = [(x * ZS + z, x * ZS + 1 - z) for x in range(XS) for z in range(ZS)]
    return lax.ppermute(value, "aux", perm)


def crossed(value, mask):
    devices = lax.axis_size("occ")
    return lax.ppermute(value, "occ", [(i, i ^ mask) for i in range(devices)])


def picked(table, index):
    hot = index[:, None] == jnp.arange(table.shape[0], dtype=jnp.int32)[None, :]
    hot = hot.reshape(hot.shape + (1,) * (table.ndim - 1))
    return jnp.sum(jnp.where(hot, table[None], 0), axis=1)


def exclusive_sum(value):
    place = jnp.arange(value.shape[-1], dtype=jnp.int32)
    ahead = place[None, :] < place[:, None]
    return jnp.sum(jnp.where(ahead, value[..., None, :], 0), axis=-1)


def row_layout(block_rows, block_order, maxrows, plane, in_plane):
    devices = block_rows.shape[0]
    numbers = jnp.arange(devices, dtype=jnp.int32)
    matches = block_order[:, None] == numbers[None, :]
    ordered = jnp.sum(jnp.where(matches, block_rows[None, :], 0), axis=1)
    starts = jnp.sum(jnp.where(matches, exclusive_sum(ordered)[:, None], 0), axis=0)
    offset = jnp.arange(DIRECT, dtype=jnp.int32)
    direct = jnp.where(offset[None, :] < block_rows[:, None], starts[:, None] + offset[None, :], -1)
    rest = jnp.maximum(block_rows - DIRECT, 0).reshape(-1, PLANE)
    first = exclusive_sum(rest)
    slots = jnp.arange(PLANE * (maxrows - DIRECT), dtype=jnp.int32)
    inside = (slots >= first[..., None]) & (slots < (first + rest)[..., None])
    source = (starts.reshape(-1, PLANE) + DIRECT - first)[..., None] + slots
    packed = jnp.sum(jnp.where(inside, source + 1, 0), axis=1) - 1
    packed = picked(packed, plane ^ jnp.arange(packed.shape[0], dtype=jnp.int32))
    targets = jnp.concatenate(
        [direct.reshape(-1), packed[:, :STEADY].reshape(-1), packed[:, STEADY:].reshape(-1)]
    )
    senders = in_plane ^ jnp.arange(PLANE, dtype=jnp.int32)
    here = jnp.reshape(plane, (1,))
    first_here, rest_here = picked(picked(first, here)[0], senders), picked(picked(rest, here)[0], senders)
    row = jnp.arange(maxrows - DIRECT, dtype=jnp.int32)
    hot = (slots[:, None, None] == first_here[:, None] + row) & (row < rest_here[:, None])
    packing = hot.reshape(slots.shape[0], -1).astype(jnp.bfloat16)
    return targets, packing, jnp.max(jnp.sum(rest, axis=1))


def table_of(targets, ao_to_virt):
    functions = jnp.arange(ao_to_virt.shape[0], dtype=jnp.int32)
    hot = (functions[:, None] == targets[None, :]).astype(jnp.bfloat16)
    return lax.dot_general(
        ao_to_virt, hot, (((0,), (0,)), ((), ())), preferred_element_type=jnp.float32
    ).astype(jnp.bfloat16)


NT = (((1,), (1,)), ((), ()))
IN_VMEM = pl.BlockSpec(memory_space=pltpu.VMEM)
IN_SMEM = pl.BlockSpec(memory_space=pltpu.SMEM)


def grant(mib):
    return pltpu.CompilerParams(vmem_limit_bytes=mib << 20)


def pack_kernel(place_ref, packing_ref, *refs):
    received, outs, rows_ref = refs[:PLANE], refs[PLANE:-1], refs[-1]
    steady, over_ref = outs[:-1], outs[-1]
    rows = received[0].shape[1]
    for step in range(len(steady)):
        plane = lax.bitwise_xor(place_ref[2], step)
        for d, ref in enumerate(received):
            rows_ref[d * rows : (d + 1) * rows, :] = ref[plane]
        packed = jnp.dot(packing_ref[...], rows_ref[...], preferred_element_type=jnp.float32)
        packed = packed.astype(rows_ref.dtype)
        steady[step][...] = packed[:STEADY]
        over_ref[step] = packed[STEADY:]


def packed_rows(place, packing, received):
    planes, rows, columns = received[0].shape
    slots = PLANE * rows
    return pl.pallas_call(
        pack_kernel,
        out_shape=[jax.ShapeDtypeStruct((STEADY, columns), jnp.bfloat16)] * planes
        + [jax.ShapeDtypeStruct((planes, slots - STEADY, columns), jnp.bfloat16)],
        in_specs=[IN_SMEM] + [IN_VMEM] * (1 + PLANE),
        out_specs=[IN_VMEM] * (planes + 1),
        scratch_shapes=[pltpu.VMEM((slots, columns), jnp.bfloat16)],
        compiler_params=grant(6),
        cost_estimate=pl.CostEstimate(
            flops=2 * planes * slots * slots * columns,
            bytes_accessed=4 * planes * slots * columns,
            transcendentals=0,
        ),
    )(place, packing, *received)


def tile_kernel(table_ref, direct_ref, *refs):
    steady, over_ref, out_ref, rows_ref = refs[:-3], refs[-3], refs[-2], refs[-1]
    count = direct_ref.shape[0]
    for step, ref in enumerate(steady):
        rows_ref[step * STEADY : (step + 1) * STEADY, :] = ref[...]
    done = len(steady) * STEADY
    rows_ref[done:, :] = over_ref[...]
    total = jnp.dot(table_ref[:, :count], direct_ref[...], preferred_element_type=jnp.float32)
    total += jnp.dot(table_ref[:, count:], rows_ref[...], preferred_element_type=jnp.float32)
    out_ref[...] = total.astype(out_ref.dtype)


def tile_of(table, direct, steady, over):
    vt, rows = table.shape
    columns = direct.shape[1]
    return pl.pallas_call(
        tile_kernel,
        out_shape=jax.ShapeDtypeStruct((vt, columns), jnp.bfloat16),
        in_specs=[IN_VMEM] * (3 + len(steady)),
        out_specs=IN_VMEM,
        scratch_shapes=[pltpu.VMEM((rows - direct.shape[0], columns), jnp.bfloat16)],
        compiler_params=grant(12),
        cost_estimate=pl.CostEstimate(
            flops=2 * vt * rows * columns,
            bytes_accessed=2 * (vt * rows + rows * columns + vt * columns),
            transcendentals=0,
        ),
    )(table, direct, *steady, over)


def own_tile_of(half_blocks, block_rows, block_order, ao_to_virt, place, position):
    maxrows, devices, columns = half_blocks.shape
    rest = maxrows - DIRECT
    planes = devices // PLANE
    plane, in_plane = position // PLANE, position % PLANE
    direct = sent_to_owners(half_blocks[:DIRECT])
    targets, packing, most = row_layout(block_rows, block_order, maxrows, plane, in_plane)
    table = table_of(targets, ao_to_virt)
    by_owner = jnp.transpose(half_blocks[DIRECT:], (1, 0, 2)).reshape(planes, PLANE, rest, columns)
    received = []
    for d in range(PLANE):
        block = lax.dynamic_index_in_dim(by_owner, in_plane ^ d, 1, keepdims=False)
        received.append(crossed(block, d) if d else block)
    *steady, over = packed_rows(place, packing, received)
    arrived = [steady[0]] + [crossed(steady[m], m * PLANE) for m in range(1, planes)]

    def overflow(rows):
        return jnp.stack([rows[0]] + [crossed(rows[m], m * PLANE) for m in range(1, planes)])

    over = lax.cond(most > STEADY, overflow, jnp.zeros_like, over)
    return tile_of(table, direct, arrived, over.reshape(-1, columns))


def sent_to_owners(rows):
    return lax.all_to_all(rows, "occ", split_axis=1, concat_axis=0, tiled=True)[:, 0, :]


def pair_kernel(own_ref, *refs):
    others, out_ref = refs[:-1], refs[-1]
    copies, _, rows, _ = out_ref.shape
    for step in range(copies):
        block = pl.ds(step * rows, rows)
        for k, other_ref in enumerate(others):
            direct = lax.dot_general(
                own_ref[block, :], other_ref[...], NT, preferred_element_type=jnp.float32
            )
            crossed = lax.dot_general(
                other_ref[block, :], own_ref[...], NT, preferred_element_type=jnp.float32
            )
            out_ref[step, k] = (2.0 * direct - crossed).astype(out_ref.dtype)


def pair_blocks(own, others):
    vt, columns = own.shape
    count = len(others)
    return pl.pallas_call(
        pair_kernel,
        out_shape=jax.ShapeDtypeStruct((XS, count, vt // XS, vt), jnp.bfloat16),
        in_specs=[IN_VMEM] * (1 + count),
        out_specs=IN_VMEM,
        compiler_params=grant(4 + 2 * count),
        cost_estimate=pl.CostEstimate(
            flops=4 * count * vt * vt * columns,
            bytes_accessed=2 * (1 + count) * vt * columns + 2 * count * vt * vt,
            transcendentals=0,
        ),
    )(own, *others)


def sum_kernel(blocks_ref, out_ref):
    total = blocks_ref[0].astype(jnp.float32)
    for step in range(1, blocks_ref.shape[0]):
        total = total + blocks_ref[step].astype(jnp.float32)
    out_ref[...] = total.astype(out_ref.dtype)


def sum_of(blocks):
    return pl.pallas_call(
        sum_kernel,
        out_shape=jax.ShapeDtypeStruct(blocks.shape[1:], jnp.bfloat16),
        in_specs=[IN_VMEM],
        out_specs=IN_VMEM,
        compiler_params=grant(4),
        cost_estimate=pl.CostEstimate(
            flops=blocks.size, bytes_accessed=3 * blocks.size, transcendentals=0
        ),
    )(blocks)


def amplitude_kernel(groups, place_ref, energy_ref, column_ref, row_ref, *refs):
    parts, out_ref = refs[:-1], refs[-1]
    copies, _, rows, _ = out_ref.shape
    occupied = energy_ref.shape[0]
    position = place_ref[0]
    block = pl.ds(pl.multiple_of(place_ref[1] * rows, rows), rows)
    both = column_ref[block, :] + row_ref[...]
    done = 0
    for group, steps in enumerate(groups):
        one_ref, two_ref = parts[2 * group : 2 * group + 2]
        for k, step in enumerate(steps):
            partner = lax.rem(position + occupied - step, occupied)
            gap = both - energy_ref[position] - energy_ref[partner]
            merged = one_ref[k].astype(jnp.float32) + two_ref[k].astype(jnp.float32)
            amplitude = (merged / gap).astype(out_ref.dtype)
            for copy in range(copies):
                out_ref[copy, done + k] = amplitude
        done += len(steps)


def amplitude_of(groups, place, energies, column, row, parts):
    count = sum(len(steps) for steps in groups)
    shape = (XS, count) + parts[0][0].shape[1:]
    size = math.prod(shape[1:])
    return pl.pallas_call(
        functools.partial(amplitude_kernel, groups),
        out_shape=jax.ShapeDtypeStruct(shape, jnp.bfloat16),
        in_specs=[IN_SMEM] * 2 + [IN_VMEM] * (2 + 2 * len(groups)),
        out_specs=IN_VMEM,
        compiler_params=grant(6),
        cost_estimate=pl.CostEstimate(
            flops=6 * size, bytes_accessed=12 * size, transcendentals=0
        ),
    )(place, energies, column, row, *[array for pair in parts for array in pair])


def density_kernel(counts, *refs):
    amplitudes, tiles = refs[: len(counts)], refs[len(counts) : len(counts) + sum(counts)]
    rest = refs[len(counts) + sum(counts) :]
    out_ref = rest[-1]
    steps, _, rows, _ = amplitudes[0].shape
    pairs = [(ref, k) for ref, count in zip(amplitudes, counts) for k in range(count)]
    for step in range(steps):
        block = pl.ds(step * rows, rows)
        total = rest[0][block, :] if len(rest) > 1 else None
        for (ref, k), tile in zip(pairs, tiles):
            term = jnp.dot(ref[step, k], tile[...], preferred_element_type=jnp.float32)
            total = term if total is None else total + term
        out_ref[block, :] = total


def density_of(amplitudes, tiles, so_far=None):
    counts = [a.shape[1] for a in amplitudes]
    count = sum(counts)
    vt, columns = tiles[0].shape
    args = list(amplitudes) + list(tiles)
    aliases = {}
    if so_far is not None:
        aliases = {len(args): 0}
        args.append(so_far)
    return pl.pallas_call(
        functools.partial(density_kernel, counts),
        out_shape=jax.ShapeDtypeStruct((vt, columns), jnp.float32),
        in_specs=[IN_VMEM] * len(args),
        out_specs=IN_VMEM,
        compiler_params=grant(12),
        input_output_aliases=aliases,
        cost_estimate=pl.CostEstimate(
            flops=2 * count * vt * vt * columns,
            bytes_accessed=4 * vt * columns + count * (2 * vt * columns + 2 * vt * vt),
            transcendentals=0,
        ),
    )(*args)


GROUPS = ((0,), (1, 2), (3,))
HALVES = ((0, 2), (2, 3))


def shards(half_blocks, block_rows, block_order, ao_to_virt, occ_energy, virt_energy):
    position = lax.axis_index("occ").astype(jnp.int32)
    place = jnp.stack(
        [position, lax.axis_index("aux").astype(jnp.int32) // ZS, position // PLANE]
    )
    column, row = virt_energy[:, None], virt_energy[None, :]
    own_tile = own_tile_of(half_blocks, block_rows, block_order, ao_to_virt, place, position)
    tiles = [own_tile, shifted(own_tile, "occ", 1), shifted(own_tile, "occ", 2)]
    tiles.append(shifted(tiles[2], "occ", 1))
    parts = []
    for steps in GROUPS:
        blocks = pair_blocks(own_tile, [tiles[k] for k in steps])
        part = sum_of(exchanged_x(blocks))
        parts.append((part, swapped_z(part)))
    density = None
    for lo, hi in HALVES:
        amplitude = amplitude_of(GROUPS[lo:hi], place, occ_energy, column, row, parts[lo:hi])
        amplitude = exchanged_x(amplitude)
        steps = [k for group in GROUPS[lo:hi] for k in group]
        density = density_of([amplitude], [tiles[k] for k in steps], density)
    return density[None]


def solution(mesh):
    return jax.shard_map(
        shards,
        mesh=mesh,
        in_specs=(P("occ", None, "aux"), P(), P(), P(), P(), P()),
        out_specs=P("occ", None, "aux"),
        check_vma=False,
    )
```

```python
import functools
import math

import jax
import jax.numpy as jnp
from jax import lax
from jax.experimental import pallas as pl
from jax.experimental.pallas import tpu as pltpu
from jax.sharding import PartitionSpec as P


XS = 4
ZS = 2
PLANE = 8
DIRECT = 8
STEADY = 80


def shifted(value, axis, by):
    devices = lax.axis_size(axis)
    return lax.ppermute(value, axis, [(i, (i + by) % devices) for i in range(devices)])


def exchanged_x(value):
    groups = [[x * ZS + z for x in range(XS)] for z in range(ZS)]
    return lax.all_to_all(value, "aux", 0, 0, axis_index_groups=groups, tiled=True)


def swapped_z(value):
    perm = [(x * ZS + z, x * ZS + 1 - z) for x in range(XS) for z in range(ZS)]
    return lax.ppermute(value, "aux", perm)


def crossed(value, mask):
    devices = lax.axis_size("occ")
    return lax.ppermute(value, "occ", [(i, i ^ mask) for i in range(devices)])


def picked(table, index):
    hot = index[:, None] == jnp.arange(table.shape[0], dtype=jnp.int32)[None, :]
    hot = hot.reshape(hot.shape + (1,) * (table.ndim - 1))
    return jnp.sum(jnp.where(hot, table[None], 0), axis=1)


def exclusive_sum(value):
    place = jnp.arange(value.shape[-1], dtype=jnp.int32)
    ahead = place[None, :] < place[:, None]
    return jnp.sum(jnp.where(ahead, value[..., None, :], 0), axis=-1)


def row_layout(block_rows, block_order, maxrows, plane):
    devices = block_rows.shape[0]
    numbers = jnp.arange(devices, dtype=jnp.int32)
    matches = block_order[:, None] == numbers[None, :]
    ordered = jnp.sum(jnp.where(matches, block_rows[None, :], 0), axis=1)
    starts = jnp.sum(jnp.where(matches, exclusive_sum(ordered)[:, None], 0), axis=0)
    offset = jnp.arange(DIRECT, dtype=jnp.int32)
    direct = jnp.where(offset[None, :] < block_rows[:, None], starts[:, None] + offset[None, :], -1)
    rest = jnp.maximum(block_rows - DIRECT, 0).reshape(-1, PLANE)
    first = exclusive_sum(rest)
    slots = jnp.arange(PLANE * (maxrows - DIRECT), dtype=jnp.int32)
    inside = (slots >= first[..., None]) & (slots < (first + rest)[..., None])
    source = (starts.reshape(-1, PLANE) + DIRECT - first)[..., None] + slots
    packed = jnp.sum(jnp.where(inside, source + 1, 0), axis=1) - 1
    packed = picked(packed, plane ^ jnp.arange(packed.shape[0], dtype=jnp.int32))
    targets = jnp.concatenate(
        [direct.reshape(-1), packed[:, :STEADY].reshape(-1), packed[:, STEADY:].reshape(-1)]
    )
    return targets, jnp.max(jnp.sum(rest, axis=1))


def table_of(targets, ao_to_virt):
    functions = jnp.arange(ao_to_virt.shape[0], dtype=jnp.int32)
    hot = (functions[:, None] == targets[None, :]).astype(jnp.bfloat16)
    return lax.dot_general(
        ao_to_virt, hot, (((0,), (0,)), ((), ())), preferred_element_type=jnp.float32
    ).astype(jnp.bfloat16)


NT = (((1,), (1,)), ((), ()))
IN_VMEM = pl.BlockSpec(memory_space=pltpu.VMEM)
IN_SMEM = pl.BlockSpec(memory_space=pltpu.SMEM)


def grant(mib):
    return pltpu.CompilerParams(vmem_limit_bytes=mib << 20)


def turn_kernel(rows_ref, out_ref):
    for low in range(0, out_ref.shape[0], PLANE):
        out_ref[low : low + PLANE] = pltpu.einshape("rdc->drc", rows_ref[:, low : low + PLANE, :])


def turned_rows(half_blocks):
    _, devices, columns = half_blocks.shape
    return pl.pallas_call(
        turn_kernel,
        grid=(1,),
        out_shape=jax.ShapeDtypeStruct((devices, DIRECT, columns), jnp.bfloat16),
        in_specs=[pl.BlockSpec((DIRECT, devices, columns), lambda i: (0, 0, 0))],
        out_specs=pl.BlockSpec((devices, DIRECT, columns), lambda i: (0, 0, 0)),
        compiler_params=grant(6),
        cost_estimate=pl.CostEstimate(
            flops=0, bytes_accessed=4 * DIRECT * devices * columns, transcendentals=0
        ),
    )(half_blocks)


def share_kernel(place_ref, rows_ref, *refs):
    outs, turned_ref = refs[:-1], refs[-1]
    planes = outs[0].shape[0]
    for plane in range(planes):
        block = rows_ref[:, plane * PLANE : (plane + 1) * PLANE, :]
        turned_ref[...] = pltpu.einshape("rdc->drc", block)
        for d, out_ref in enumerate(outs):
            out_ref[plane] = turned_ref[lax.bitwise_xor(place_ref[3], d)]


def shared_rows(place, rows):
    count, devices, columns = rows.shape
    return pl.pallas_call(
        share_kernel,
        out_shape=[
            jax.ShapeDtypeStruct((devices // PLANE, count, columns), jnp.bfloat16)
        ] * PLANE,
        in_specs=[IN_SMEM, IN_VMEM],
        out_specs=[IN_VMEM] * PLANE,
        scratch_shapes=[pltpu.VMEM((PLANE, count, columns), jnp.bfloat16)],
        compiler_params=grant(8),
        cost_estimate=pl.CostEstimate(flops=0, bytes_accessed=4 * rows.size, transcendentals=0),
    )(place, rows)


def pack_kernel(place_ref, counts_ref, *refs):
    received, outs = refs[:PLANE], refs[PLANE:-2]
    rows_ref, first_ref = refs[-2:]
    steady, over_ref = outs[:-1], outs[-1]
    rows = received[0].shape[1]
    here = place_ref[2] * PLANE
    so_far = jnp.int32(0)
    for member in range(PLANE):
        first_ref[member] = so_far
        so_far += jnp.maximum(counts_ref[here + member] - DIRECT, 0)
    slots = rows_ref.shape[0]
    slot = lax.broadcasted_iota(jnp.int32, (slots, slots), 0)
    column = lax.broadcasted_iota(jnp.int32, (slots, slots), 1)
    wanted = jnp.full((slots, slots), -1, jnp.int32)
    for d in range(PLANE):
        sender = lax.bitwise_xor(place_ref[3], d)
        row = column - d * rows
        held = (row >= 0) & (row < jnp.minimum(counts_ref[here + sender] - DIRECT, rows))
        wanted = jnp.where(held, first_ref[sender] + row, wanted)
    packing = jnp.where(slot == wanted, 1.0, 0.0).astype(rows_ref.dtype)
    for step in range(len(steady)):
        plane = lax.bitwise_xor(place_ref[2], step)
        for d, ref in enumerate(received):
            rows_ref[d * rows : (d + 1) * rows, :] = ref[plane]
        packed = jnp.dot(packing, rows_ref[...], preferred_element_type=jnp.float32)
        packed = packed.astype(rows_ref.dtype)
        steady[step][...] = packed[:STEADY]
        over_ref[step] = packed[STEADY:]


def packed_rows(place, counts, received):
    planes, rows, columns = received[0].shape
    slots = PLANE * rows
    return pl.pallas_call(
        pack_kernel,
        out_shape=[jax.ShapeDtypeStruct((STEADY, columns), jnp.bfloat16)] * planes
        + [jax.ShapeDtypeStruct((planes, slots - STEADY, columns), jnp.bfloat16)],
        in_specs=[IN_SMEM] * 2 + [IN_VMEM] * PLANE,
        out_specs=[IN_VMEM] * (planes + 1),
        scratch_shapes=[
            pltpu.VMEM((slots, columns), jnp.bfloat16),
            pltpu.SMEM((PLANE,), jnp.int32),
        ],
        compiler_params=grant(6),
        cost_estimate=pl.CostEstimate(
            flops=2 * planes * slots * slots * columns,
            bytes_accessed=4 * planes * slots * columns,
            transcendentals=0,
        ),
    )(place, counts, *received)


def tile_kernel(table_ref, direct_ref, *refs):
    steady, over_ref, out_ref, rows_ref = refs[:-3], refs[-3], refs[-2], refs[-1]
    count = direct_ref.shape[0]
    for step, ref in enumerate(steady):
        rows_ref[step * STEADY : (step + 1) * STEADY, :] = ref[...]
    done = len(steady) * STEADY
    rows_ref[done:, :] = over_ref[...]
    total = jnp.dot(table_ref[:, :count], direct_ref[...], preferred_element_type=jnp.float32)
    total += jnp.dot(table_ref[:, count:], rows_ref[...], preferred_element_type=jnp.float32)
    out_ref[...] = total.astype(out_ref.dtype)


def tile_of(table, direct, steady, over):
    vt, rows = table.shape
    columns = direct.shape[1]
    return pl.pallas_call(
        tile_kernel,
        out_shape=jax.ShapeDtypeStruct((vt, columns), jnp.bfloat16),
        in_specs=[IN_VMEM] * (3 + len(steady)),
        out_specs=IN_VMEM,
        scratch_shapes=[pltpu.VMEM((rows - direct.shape[0], columns), jnp.bfloat16)],
        compiler_params=grant(56),
        cost_estimate=pl.CostEstimate(
            flops=2 * vt * rows * columns,
            bytes_accessed=2 * (vt * rows + rows * columns + vt * columns),
            transcendentals=0,
        ),
    )(table, direct, *steady, over)


def own_tile_of(half_blocks, block_rows, block_order, ao_to_virt, place, position):
    maxrows, devices, columns = half_blocks.shape
    planes = devices // PLANE
    plane = position // PLANE
    direct = sent_to_owners(turned_rows(half_blocks))
    targets, most = row_layout(block_rows, block_order, maxrows, plane)
    table = table_of(targets, ao_to_virt)
    blocks = shared_rows(place, half_blocks[DIRECT:])
    received = [blocks[0]] + [crossed(blocks[d], d) for d in range(1, PLANE)]
    *steady, over = packed_rows(place, block_rows, received)
    arrived = [steady[0]] + [None] * (planes - 1)
    for m in sorted(range(1, planes), key=lambda m: (m < planes // 2, m)):
        arrived[m] = crossed(steady[m], m * PLANE)

    def overflow(rows):
        return jnp.stack([rows[0]] + [crossed(rows[m], m * PLANE) for m in range(1, planes)])

    over = lax.cond(most > STEADY, overflow, jnp.zeros_like, over)
    return tile_of(table, direct, arrived, over.reshape(-1, columns))


def sent_to_owners(rows):
    arrived = lax.all_to_all(rows, "occ", split_axis=0, concat_axis=0, tiled=True)
    return arrived.reshape(-1, rows.shape[2])


def pair_kernel(own_ref, *refs):
    others, out_ref = refs[:-1], refs[-1]
    copies, _, rows, _ = out_ref.shape
    for step in range(copies):
        block = pl.ds(step * rows, rows)
        for k, other_ref in enumerate(others):
            direct = lax.dot_general(
                own_ref[block, :], other_ref[...], NT, preferred_element_type=jnp.float32
            )
            crossed = lax.dot_general(
                other_ref[block, :], own_ref[...], NT, preferred_element_type=jnp.float32
            )
            out_ref[step, k] = (2.0 * direct - crossed).astype(out_ref.dtype)


def pair_blocks(own, others):
    vt, columns = own.shape
    count = len(others)
    return pl.pallas_call(
        pair_kernel,
        out_shape=jax.ShapeDtypeStruct((XS, count, vt // XS, vt), jnp.bfloat16),
        in_specs=[IN_VMEM] * (1 + count),
        out_specs=IN_VMEM,
        compiler_params=grant(4 + 2 * count),
        cost_estimate=pl.CostEstimate(
            flops=4 * count * vt * vt * columns,
            bytes_accessed=2 * (1 + count) * vt * columns + 2 * count * vt * vt,
            transcendentals=0,
        ),
    )(own, *others)


def sum_kernel(blocks_ref, out_ref):
    total = blocks_ref[0].astype(jnp.float32)
    for step in range(1, blocks_ref.shape[0]):
        total = total + blocks_ref[step].astype(jnp.float32)
    out_ref[...] = total.astype(out_ref.dtype)


def sum_of(blocks):
    return pl.pallas_call(
        sum_kernel,
        out_shape=jax.ShapeDtypeStruct(blocks.shape[1:], jnp.bfloat16),
        in_specs=[IN_VMEM],
        out_specs=IN_VMEM,
        compiler_params=grant(4),
        cost_estimate=pl.CostEstimate(
            flops=blocks.size, bytes_accessed=3 * blocks.size, transcendentals=0
        ),
    )(blocks)


def amplitude_kernel(groups, place_ref, energy_ref, column_ref, row_ref, *refs):
    parts, out_ref = refs[:-1], refs[-1]
    copies, _, rows, _ = out_ref.shape
    occupied = energy_ref.shape[0]
    position = place_ref[0]
    block = pl.ds(pl.multiple_of(place_ref[1] * rows, rows), rows)
    both = column_ref[block, :] + row_ref[...]
    done = 0
    for group, steps in enumerate(groups):
        one_ref, two_ref = parts[2 * group : 2 * group + 2]
        for k, step in enumerate(steps):
            partner = lax.rem(position + occupied - step, occupied)
            gap = both - energy_ref[position] - energy_ref[partner]
            merged = one_ref[k].astype(jnp.float32) + two_ref[k].astype(jnp.float32)
            amplitude = (merged / gap).astype(out_ref.dtype)
            for copy in range(copies):
                out_ref[copy, done + k] = amplitude
        done += len(steps)


def amplitude_of(groups, place, energies, column, row, parts):
    count = sum(len(steps) for steps in groups)
    shape = (XS, count) + parts[0][0].shape[1:]
    size = math.prod(shape[1:])
    return pl.pallas_call(
        functools.partial(amplitude_kernel, groups),
        out_shape=jax.ShapeDtypeStruct(shape, jnp.bfloat16),
        in_specs=[IN_SMEM] * 2 + [IN_VMEM] * (2 + 2 * len(groups)),
        out_specs=IN_VMEM,
        compiler_params=grant(6),
        cost_estimate=pl.CostEstimate(
            flops=6 * size, bytes_accessed=12 * size, transcendentals=0
        ),
    )(place, energies, column, row, *[array for pair in parts for array in pair])


def density_kernel(count, amplitude_ref, *refs):
    tiles, rest = refs[:count], refs[count:]
    tile_ref, sems = rest[-2:]
    out_ref = rest[-3]
    copies = [pltpu.make_async_copy(tiles[k], tile_ref.at[k], sems.at[k]) for k in range(count)]
    for copy in copies:
        copy.start()
    for copy in copies:
        copy.wait()
    steps, _, rows, _ = amplitude_ref.shape
    for step in range(steps):
        block = pl.ds(step * rows, rows)
        total = rest[0][block, :] if len(rest) > 3 else None
        for k in range(count):
            term = jnp.dot(
                amplitude_ref[step, k], tile_ref[k], preferred_element_type=jnp.float32
            )
            total = term if total is None else total + term
        out_ref[block, :] = total


def density_of(amplitudes, tiles, so_far=None):
    count = len(tiles)
    vt, columns = tiles[0].shape
    args = [amplitudes] + list(tiles)
    in_specs = [IN_VMEM] + [pl.BlockSpec(memory_space=pltpu.HBM)] * count
    aliases = {}
    if so_far is not None:
        aliases = {len(args): 0}
        args.append(so_far)
        in_specs.append(IN_VMEM)
    return pl.pallas_call(
        functools.partial(density_kernel, count),
        out_shape=jax.ShapeDtypeStruct((vt, columns), jnp.float32),
        in_specs=in_specs,
        out_specs=IN_VMEM,
        scratch_shapes=[
            pltpu.VMEM((count, vt, columns), jnp.bfloat16),
            pltpu.SemaphoreType.DMA((count,)),
        ],
        compiler_params=grant(14),
        input_output_aliases=aliases,
        cost_estimate=pl.CostEstimate(
            flops=2 * count * vt * vt * columns,
            bytes_accessed=4 * vt * columns + count * (2 * vt * columns + 2 * vt * vt),
            transcendentals=0,
        ),
    )(*args)


GROUPS = ((0,), (1, 2), (3,))
HALVES = ((0, 2), (2, 3))


def shards(half_blocks, block_rows, block_order, ao_to_virt, occ_energy, virt_energy):
    position = lax.axis_index("occ").astype(jnp.int32)
    place = jnp.stack(
        [
            position,
            lax.axis_index("aux").astype(jnp.int32) // ZS,
            position // PLANE,
            position % PLANE,
        ]
    )
    column, row = virt_energy[:, None], virt_energy[None, :]
    own_tile = own_tile_of(half_blocks, block_rows, block_order, ao_to_virt, place, position)
    tiles = [own_tile, shifted(own_tile, "occ", 1), shifted(own_tile, "occ", 2)]
    tiles.append(shifted(tiles[2], "occ", 1))
    parts = []
    for steps in GROUPS:
        blocks = pair_blocks(own_tile, [tiles[k] for k in steps])
        part = sum_of(exchanged_x(blocks))
        parts.append((part, swapped_z(part)))
    density = None
    for lo, hi in HALVES:
        amplitude = amplitude_of(GROUPS[lo:hi], place, occ_energy, column, row, parts[lo:hi])
        amplitude = exchanged_x(amplitude)
        steps = [k for group in GROUPS[lo:hi] for k in group]
        density = density_of(amplitude, [tiles[k] for k in steps], density)
    return density[None]


def solution(mesh):
    return jax.shard_map(
        shards,
        mesh=mesh,
        in_specs=(P("occ", None, "aux"), P(), P(), P(), P(), P()),
        out_specs=P("occ", None, "aux"),
        check_vma=False,
    )
```

```python
import functools
import math

import jax
import jax.numpy as jnp
from jax import lax
from jax.experimental import pallas as pl
from jax.experimental.pallas import tpu as pltpu
from jax.sharding import PartitionSpec as P


XS = 4
ZS = 2
PLANE = 8
DIRECT = 8
STEADY = 88


def shifted(value, axis, by):
    devices = lax.axis_size(axis)
    return lax.ppermute(value, axis, [(i, (i + by) % devices) for i in range(devices)])


def exchanged_x(value):
    groups = [[x * ZS + z for x in range(XS)] for z in range(ZS)]
    return lax.all_to_all(value, "aux", 0, 0, axis_index_groups=groups, tiled=True)


def swapped_z(value):
    perm = [(x * ZS + z, x * ZS + 1 - z) for x in range(XS) for z in range(ZS)]
    return lax.ppermute(value, "aux", perm)


def crossed(value, mask):
    devices = lax.axis_size("occ")
    return lax.ppermute(value, "occ", [(i, i ^ mask) for i in range(devices)])


def picked(table, index):
    hot = index[:, None] == jnp.arange(table.shape[0], dtype=jnp.int32)[None, :]
    hot = hot.reshape(hot.shape + (1,) * (table.ndim - 1))
    return jnp.sum(jnp.where(hot, table[None], 0), axis=1)


def exclusive_sum(value):
    place = jnp.arange(value.shape[-1], dtype=jnp.int32)
    ahead = place[None, :] < place[:, None]
    return jnp.sum(jnp.where(ahead, value[..., None, :], 0), axis=-1)


def row_layout(block_rows, block_order, maxrows, plane):
    devices = block_rows.shape[0]
    numbers = jnp.arange(devices, dtype=jnp.int32)
    matches = block_order[:, None] == numbers[None, :]
    ordered = jnp.sum(jnp.where(matches, block_rows[None, :], 0), axis=1)
    starts = jnp.sum(jnp.where(matches, exclusive_sum(ordered)[:, None], 0), axis=0)
    offset = jnp.arange(DIRECT, dtype=jnp.int32)
    direct = jnp.where(offset[None, :] < block_rows[:, None], starts[:, None] + offset[None, :], -1)
    rest = jnp.maximum(block_rows - DIRECT, 0).reshape(-1, PLANE)
    first = exclusive_sum(rest)
    slots = jnp.arange(PLANE * (maxrows - DIRECT), dtype=jnp.int32)
    inside = (slots >= first[..., None]) & (slots < (first + rest)[..., None])
    source = (starts.reshape(-1, PLANE) + DIRECT - first)[..., None] + slots
    packed = jnp.sum(jnp.where(inside, source + 1, 0), axis=1) - 1
    packed = picked(packed, plane ^ jnp.arange(packed.shape[0], dtype=jnp.int32))
    targets = jnp.concatenate(
        [direct.reshape(-1), packed[:, :STEADY].reshape(-1), packed[:, STEADY:].reshape(-1)]
    )
    return targets, jnp.max(jnp.sum(rest, axis=1))


def table_of(targets, ao_to_virt):
    functions = jnp.arange(ao_to_virt.shape[0], dtype=jnp.int32)
    hot = (functions[:, None] == targets[None, :]).astype(jnp.bfloat16)
    return lax.dot_general(
        ao_to_virt, hot, (((0,), (0,)), ((), ())), preferred_element_type=jnp.float32
    ).astype(jnp.bfloat16)


NT = (((1,), (1,)), ((), ()))
IN_VMEM = pl.BlockSpec(memory_space=pltpu.VMEM)
IN_SMEM = pl.BlockSpec(memory_space=pltpu.SMEM)


def grant(mib):
    return pltpu.CompilerParams(vmem_limit_bytes=mib << 20)


def turn_kernel(rows_ref, out_ref):
    for low in range(0, out_ref.shape[0], PLANE):
        out_ref[low : low + PLANE] = pltpu.einshape("rdc->drc", rows_ref[:, low : low + PLANE, :])


def turned_rows(half_blocks):
    _, devices, columns = half_blocks.shape
    return pl.pallas_call(
        turn_kernel,
        grid=(1,),
        out_shape=jax.ShapeDtypeStruct((devices, DIRECT, columns), jnp.bfloat16),
        in_specs=[pl.BlockSpec((DIRECT, devices, columns), lambda i: (0, 0, 0))],
        out_specs=pl.BlockSpec((devices, DIRECT, columns), lambda i: (0, 0, 0)),
        compiler_params=grant(6),
        cost_estimate=pl.CostEstimate(
            flops=0, bytes_accessed=4 * DIRECT * devices * columns, transcendentals=0
        ),
    )(half_blocks)


def share_kernel(place_ref, rows_ref, *refs):
    outs, turned_ref = refs[:-1], refs[-1]
    planes = outs[0].shape[0]
    for plane in range(planes):
        block = rows_ref[:, plane * PLANE : (plane + 1) * PLANE, :]
        turned_ref[...] = pltpu.einshape("rdc->drc", block)
        for d, out_ref in enumerate(outs):
            out_ref[plane] = turned_ref[lax.bitwise_xor(place_ref[3], d)]


def shared_rows(place, rows):
    count, devices, columns = rows.shape
    return pl.pallas_call(
        share_kernel,
        out_shape=[
            jax.ShapeDtypeStruct((devices // PLANE, count, columns), jnp.bfloat16)
        ] * PLANE,
        in_specs=[IN_SMEM, IN_VMEM],
        out_specs=[IN_VMEM] * PLANE,
        scratch_shapes=[pltpu.VMEM((PLANE, count, columns), jnp.bfloat16)],
        compiler_params=grant(8),
        cost_estimate=pl.CostEstimate(flops=0, bytes_accessed=4 * rows.size, transcendentals=0),
    )(place, rows)


def pack_kernel(place_ref, counts_ref, *refs):
    received, outs = refs[:PLANE], refs[PLANE:-2]
    rows_ref, first_ref = refs[-2:]
    steady, over_ref = outs[:-1], outs[-1]
    rows = received[0].shape[1]
    here = place_ref[2] * PLANE
    so_far = jnp.int32(0)
    for member in range(PLANE):
        first_ref[member] = so_far
        so_far += jnp.maximum(counts_ref[here + member] - DIRECT, 0)
    slots = rows_ref.shape[0]
    slot = lax.broadcasted_iota(jnp.int32, (slots, slots), 0)
    column = lax.broadcasted_iota(jnp.int32, (slots, slots), 1)
    wanted = jnp.full((slots, slots), -1, jnp.int32)
    for d in range(PLANE):
        sender = lax.bitwise_xor(place_ref[3], d)
        row = column - d * rows
        held = (row >= 0) & (row < jnp.minimum(counts_ref[here + sender] - DIRECT, rows))
        wanted = jnp.where(held, first_ref[sender] + row, wanted)
    packing = jnp.where(slot == wanted, 1.0, 0.0).astype(rows_ref.dtype)
    for step in range(len(steady)):
        plane = lax.bitwise_xor(place_ref[2], step)
        for d, ref in enumerate(received):
            rows_ref[d * rows : (d + 1) * rows, :] = ref[plane]
        packed = jnp.dot(packing, rows_ref[...], preferred_element_type=jnp.float32)
        packed = packed.astype(rows_ref.dtype)
        steady[step][...] = packed[:STEADY]
        over_ref[step] = packed[STEADY:]


def packed_rows(place, counts, received):
    planes, rows, columns = received[0].shape
    slots = PLANE * rows
    return pl.pallas_call(
        pack_kernel,
        out_shape=[jax.ShapeDtypeStruct((STEADY, columns), jnp.bfloat16)] * planes
        + [jax.ShapeDtypeStruct((planes, slots - STEADY, columns), jnp.bfloat16)],
        in_specs=[IN_SMEM] * 2 + [IN_VMEM] * PLANE,
        out_specs=[IN_VMEM] * (planes + 1),
        scratch_shapes=[
            pltpu.VMEM((slots, columns), jnp.bfloat16),
            pltpu.SMEM((PLANE,), jnp.int32),
        ],
        compiler_params=grant(6),
        cost_estimate=pl.CostEstimate(
            flops=2 * planes * slots * slots * columns,
            bytes_accessed=4 * planes * slots * columns,
            transcendentals=0,
        ),
    )(place, counts, *received)


def tile_kernel(table_ref, direct_ref, *refs):
    steady, over_ref, out_ref, rows_ref = refs[:-3], refs[-3], refs[-2], refs[-1]
    count = direct_ref.shape[0]
    for step, ref in enumerate(steady):
        rows_ref[step * STEADY : (step + 1) * STEADY, :] = ref[...]
    done = len(steady) * STEADY
    rows_ref[done:, :] = over_ref[...]
    total = jnp.dot(table_ref[:, :count], direct_ref[...], preferred_element_type=jnp.float32)
    total += jnp.dot(table_ref[:, count:], rows_ref[...], preferred_element_type=jnp.float32)
    out_ref[...] = total.astype(out_ref.dtype)


def tile_of(table, direct, steady, over):
    vt, rows = table.shape
    columns = direct.shape[1]
    return pl.pallas_call(
        tile_kernel,
        out_shape=jax.ShapeDtypeStruct((vt, columns), jnp.bfloat16),
        in_specs=[IN_VMEM] * (3 + len(steady)),
        out_specs=IN_VMEM,
        scratch_shapes=[pltpu.VMEM((rows - direct.shape[0], columns), jnp.bfloat16)],
        compiler_params=grant(56),
        cost_estimate=pl.CostEstimate(
            flops=2 * vt * rows * columns,
            bytes_accessed=2 * (vt * rows + rows * columns + vt * columns),
            transcendentals=0,
        ),
    )(table, direct, *steady, over)


def own_tile_of(half_blocks, block_rows, block_order, ao_to_virt, place, position):
    maxrows, devices, columns = half_blocks.shape
    planes = devices // PLANE
    plane = position // PLANE
    direct = sent_to_owners(turned_rows(half_blocks))
    targets, most = row_layout(block_rows, block_order, maxrows, plane)
    table = table_of(targets, ao_to_virt)
    blocks = shared_rows(place, half_blocks[DIRECT:])
    received = [blocks[0]] + [crossed(blocks[d], d) for d in range(1, PLANE)]
    *steady, over = packed_rows(place, block_rows, received)
    arrived = [steady[0]] + [None] * (planes - 1)
    for m in sorted(range(1, planes), key=lambda m: (m < planes // 2, m)):
        arrived[m] = crossed(steady[m], m * PLANE)

    def overflow(rows):
        return jnp.stack([rows[0]] + [crossed(rows[m], m * PLANE) for m in range(1, planes)])

    over = lax.cond(most > STEADY, overflow, jnp.zeros_like, over)
    return tile_of(table, direct, arrived, over.reshape(-1, columns))


def sent_to_owners(rows):
    arrived = lax.all_to_all(rows, "occ", split_axis=0, concat_axis=0, tiled=True)
    return arrived.reshape(-1, rows.shape[2])


def pair_kernel(own_ref, *refs):
    others, out_ref = refs[:-1], refs[-1]
    copies, _, rows, _ = out_ref.shape
    for k, other_ref in enumerate(others):
        direct = lax.dot_general(
            own_ref[...], other_ref[...], NT, preferred_element_type=jnp.float32
        )
        crossed_over = lax.dot_general(
            other_ref[...], own_ref[...], NT, preferred_element_type=jnp.float32
        )
        value = (2.0 * direct - crossed_over).astype(out_ref.dtype)
        for step in range(copies):
            out_ref[step, k] = value[step * rows : (step + 1) * rows]


def pair_blocks(own, others):
    vt, columns = own.shape
    count = len(others)
    return pl.pallas_call(
        pair_kernel,
        out_shape=jax.ShapeDtypeStruct((XS, count, vt // XS, vt), jnp.bfloat16),
        in_specs=[IN_VMEM] * (1 + count),
        out_specs=IN_VMEM,
        compiler_params=grant(4 + 2 * count),
        cost_estimate=pl.CostEstimate(
            flops=4 * count * vt * vt * columns,
            bytes_accessed=2 * (1 + count) * vt * columns + 2 * count * vt * vt,
            transcendentals=0,
        ),
    )(own, *others)


def sum_kernel(blocks_ref, out_ref):
    total = blocks_ref[0].astype(jnp.float32)
    for step in range(1, blocks_ref.shape[0]):
        total = total + blocks_ref[step].astype(jnp.float32)
    out_ref[...] = total.astype(out_ref.dtype)


def sum_of(blocks):
    return pl.pallas_call(
        sum_kernel,
        out_shape=jax.ShapeDtypeStruct(blocks.shape[1:], jnp.bfloat16),
        in_specs=[IN_VMEM],
        out_specs=IN_VMEM,
        compiler_params=grant(4),
        cost_estimate=pl.CostEstimate(
            flops=blocks.size, bytes_accessed=3 * blocks.size, transcendentals=0
        ),
    )(blocks)


def amplitude_kernel(groups, place_ref, energy_ref, column_ref, row_ref, *refs):
    parts, out_ref = refs[:-1], refs[-1]
    copies, _, rows, _ = out_ref.shape
    occupied = energy_ref.shape[0]
    position = place_ref[0]
    block = pl.ds(pl.multiple_of(place_ref[1] * rows, rows), rows)
    both = column_ref[block, :] + row_ref[...]
    done = 0
    for group, steps in enumerate(groups):
        one_ref, two_ref = parts[2 * group : 2 * group + 2]
        for k, step in enumerate(steps):
            partner = lax.rem(position + occupied - step, occupied)
            gap = both - energy_ref[position] - energy_ref[partner]
            merged = one_ref[k].astype(jnp.float32) + two_ref[k].astype(jnp.float32)
            amplitude = (merged / gap).astype(out_ref.dtype)
            for copy in range(copies):
                out_ref[copy, done + k] = amplitude
        done += len(steps)


def amplitude_of(groups, place, energies, column, row, parts):
    count = sum(len(steps) for steps in groups)
    shape = (XS, count) + parts[0][0].shape[1:]
    size = math.prod(shape[1:])
    return pl.pallas_call(
        functools.partial(amplitude_kernel, groups),
        out_shape=jax.ShapeDtypeStruct(shape, jnp.bfloat16),
        in_specs=[IN_SMEM] * 2 + [IN_VMEM] * (2 + 2 * len(groups)),
        out_specs=IN_VMEM,
        compiler_params=grant(6),
        cost_estimate=pl.CostEstimate(
            flops=6 * size, bytes_accessed=12 * size, transcendentals=0
        ),
    )(place, energies, column, row, *[array for pair in parts for array in pair])


def density_kernel(count, amplitude_ref, *refs):
    tiles, rest = refs[:count], refs[count:]
    tile_ref, sems = rest[-2:]
    out_ref = rest[-3]
    copies = [pltpu.make_async_copy(tiles[k], tile_ref.at[k], sems.at[k]) for k in range(count)]
    for copy in copies:
        copy.start()
    for copy in copies:
        copy.wait()
    vt = out_ref.shape[0]
    total = rest[0][...] if len(rest) > 3 else None
    for k in range(count):
        term = jnp.dot(
            amplitude_ref[:, k].reshape(vt, vt), tile_ref[k], preferred_element_type=jnp.float32
        )
        total = term if total is None else total + term
    out_ref[...] = total


def density_of(amplitudes, tiles, so_far=None):
    count = len(tiles)
    vt, columns = tiles[0].shape
    args = [amplitudes] + list(tiles)
    in_specs = [IN_VMEM] + [pl.BlockSpec(memory_space=pltpu.HBM)] * count
    aliases = {}
    if so_far is not None:
        aliases = {len(args): 0}
        args.append(so_far)
        in_specs.append(IN_VMEM)
    return pl.pallas_call(
        functools.partial(density_kernel, count),
        out_shape=jax.ShapeDtypeStruct((vt, columns), jnp.float32),
        in_specs=in_specs,
        out_specs=IN_VMEM,
        scratch_shapes=[
            pltpu.VMEM((count, vt, columns), jnp.bfloat16),
            pltpu.SemaphoreType.DMA((count,)),
        ],
        compiler_params=grant(14),
        input_output_aliases=aliases,
        cost_estimate=pl.CostEstimate(
            flops=2 * count * vt * vt * columns,
            bytes_accessed=4 * vt * columns + count * (2 * vt * columns + 2 * vt * vt),
            transcendentals=0,
        ),
    )(*args)


GROUPS = ((0,), (1, 2), (3,))
HALVES = ((0, 2), (2, 3))


def shards(half_blocks, block_rows, block_order, ao_to_virt, occ_energy, virt_energy):
    position = lax.axis_index("occ").astype(jnp.int32)
    place = jnp.stack(
        [
            position,
            lax.axis_index("aux").astype(jnp.int32) // ZS,
            position // PLANE,
            position % PLANE,
        ]
    )
    column, row = virt_energy[:, None], virt_energy[None, :]
    own_tile = own_tile_of(half_blocks, block_rows, block_order, ao_to_virt, place, position)
    tiles = [own_tile, shifted(own_tile, "occ", 1), shifted(own_tile, "occ", 2)]
    tiles.append(shifted(tiles[2], "occ", 1))
    parts = []
    for steps in GROUPS:
        blocks = pair_blocks(own_tile, [tiles[k] for k in steps])
        part = sum_of(exchanged_x(blocks))
        parts.append((part, swapped_z(part)))
    density = None
    for lo, hi in HALVES:
        amplitude = amplitude_of(GROUPS[lo:hi], place, occ_energy, column, row, parts[lo:hi])
        amplitude = exchanged_x(amplitude)
        steps = [k for group in GROUPS[lo:hi] for k in group]
        density = density_of(amplitude, [tiles[k] for k in steps], density)
    return density[None]


def solution(mesh):
    return jax.shard_map(
        shards,
        mesh=mesh,
        in_specs=(P("occ", None, "aux"), P(), P(), P(), P(), P()),
        out_specs=P("occ", None, "aux"),
        check_vma=False,
    )
```
